32 devices in a mesh: groups: 2 (over x), seq: 16 (over z, y, core).
Axes of the slice: x: 2, y: 2, z: 4, core: 2. Of those that a mesh axis runs over, the one named last changes fastest.
Arguments:
- video: bfloat16 [32, 256, 1152], P(('groups', 'seq')), parts along dimension 0, may hold values from -6 to 6
- spatial_qkv: bfloat16 [1152, 3456], P(None, 'seq'), may hold values from -0.53033009 to 0.53033009
- spatial_out: bfloat16 [1152, 1152], P(None, 'seq'), may hold values from -0.1875 to 0.1875
- temporal_qkv: bfloat16 [1152, 3456], P(None, 'seq'), may hold values from -0.53033009 to 0.53033009
- temporal_out: bfloat16 [1152, 1152], P(None, 'seq'), may hold values from -0.1875 to 0.1875
Outputs:
- video_out: bfloat16 [32, 256, 1152], P(('groups', 'seq')), parts along dimension 0
The draws below stay inside these ranges and needn't reach their ends.
There are 2 independent parts, one for each index of `groups`. The reference program is written for one: setup_inputs(seed, part) draws one part's arguments, and reference() takes and returns one part's arrays. A program takes and returns all parts, laid end to end along the dimension named above; an argument that names none is the same for every part. Nothing has to cross between parts.
All inputs are finite; a program needn't handle non-finite values.
Results may differ from the reference program's by a relative error of at most 0.023.
The reference program's roundings to bfloat16 on the way count: a program that leaves them out, or rounds other values in their place, can miss the bound.
Values may be sent and summed in bfloat16 or wider, within the bound.
A program may use at most 128 MiB of HBM per device.

```python
import math
import jax
import jax.numpy as jnp
from jax import lax

D = 1152
HEADS = 16
PATCHES = 256
FRAMES = 16


def qkv_table(key):
    deviation = D ** (-0.5)
    base = jax.random.truncated_normal(key, -4.0, 4.0, (D, 3 * D), jnp.float32) * deviation
    boost = 1.0
    column = lax.broadcasted_iota(jnp.int32, (1, 3 * D), 1)
    factor = jnp.where(column < 2 * D, boost, 1.0)
    return base * factor


def draw_spatial_qkv(key, part):
    return qkv_table(jax.random.fold_in(key, 11)).astype(jnp.bfloat16)


def draw_temporal_qkv(key, part):
    return qkv_table(jax.random.fold_in(key, 29)).astype(jnp.bfloat16)


def level_of(own_key, shape, shards, least, top_value):
    gain, own = 1.0, jax.random.fold_in(own_key, 6)
    for axis_at, blocks in shards:
        heights = jnp.exp(jax.random.uniform(jax.random.fold_in(own, axis_at), (blocks,), jnp.float32, least / len(shards), top_value / len(shards)))
        gain = gain * jnp.repeat(heights, shape[axis_at] // blocks).reshape([-1 if axis == axis_at else 1 for axis in range(len(shape))])
    return gain


def bell_draw(key, extent, scale, reach, shards=(), kind=jnp.bfloat16):
    values = jax.random.normal(key, extent, jnp.float32) * scale
    if len(shards) > 0:
        values = level_of(key, extent, shards, -0.22, 0.18) * values
    return jnp.clip(values, min=-reach, max=reach).astype(kind)


def setup_inputs(seed: int = 0, part: int = 0) -> dict:
    splits = jax.random.split(jax.random.key(seed), 6)
    own_keys = jax.random.split(jax.random.fold_in(splits[5], part), 6)
    return {
        "video": bell_draw(own_keys[0], (FRAMES, PATCHES, D), 1.0, 6.0, ((0, 16),)),
        "spatial_qkv": draw_spatial_qkv(jax.random.fold_in(splits[5], 71), part),
        "spatial_out": bell_draw(splits[2], (D, D), D ** -0.5, 0.1875, ((1, 16),)),
        "temporal_qkv": draw_temporal_qkv(jax.random.fold_in(splits[5], 71), part),
        "temporal_out": bell_draw(splits[4], (D, D), D ** -0.5, 0.1875, ((1, 16),)),
    }


epsilon = 1e-06

def normalize(values):
    average = lax.optimization_barrier(jnp.mean(values, axis=-1, keepdims=True))
    centered = values - average
    spread = lax.optimization_barrier(jnp.mean(centered * centered, axis=-1, keepdims=True))
    return (centered * lax.rsqrt(spread + epsilon)).astype(jnp.bfloat16)

def split_heads(table, leading, second, which):
    width = table.shape[1] // 3
    block = table[:, which * width:(which + 1) * width]
    return block.reshape(leading, second, HEADS, width // HEADS)

def attend(queries, key_rows, value_rows, score_form, mix_form):
    head_width = queries.shape[-1]

    def one_head(parts):
        head_query, head_key, head_value = parts
        scores = jnp.einsum(score_form, head_query.astype(jnp.float32), head_key.astype(jnp.float32)) / math.sqrt(head_width)
        highest = lax.optimization_barrier(jnp.max(scores, axis=-1, keepdims=True))
        powers = jnp.exp(scores - highest)
        probs = (powers / lax.optimization_barrier(jnp.sum(powers, axis=-1, keepdims=True))).astype(jnp.bfloat16)
        return jnp.einsum(mix_form, probs.astype(jnp.float32), head_value.astype(jnp.float32)).astype(jnp.bfloat16)
    stacked = lax.map(one_head, (jnp.moveaxis(queries, 2, 0), jnp.moveaxis(key_rows, 2, 0), jnp.moveaxis(value_rows, 2, 0)))
    moved = jnp.moveaxis(stacked, 0, 2)
    return moved.reshape(moved.shape[0], moved.shape[1], -1)

def sublayer(tokens, qkv_weight, out_weight, score_form, mix_form):
    frames, patches, width = tokens.shape
    rows = tokens.reshape(frames * patches, width)
    normed = normalize(rows.astype(jnp.float32))
    table = jnp.dot(normed, qkv_weight, preferred_element_type=jnp.float32).astype(jnp.bfloat16)
    mixed = attend(split_heads(table, frames, patches, 0), split_heads(table, frames, patches, 1), split_heads(table, frames, patches, 2), score_form, mix_form)
    update = jnp.dot(mixed.reshape(frames * patches, width), out_weight, preferred_element_type=jnp.float32)
    return (rows.astype(jnp.float32) + update).astype(jnp.bfloat16).reshape(frames, patches, width)

def reference(video, spatial_qkv, spatial_out, temporal_qkv, temporal_out):
    hidden = sublayer(video, spatial_qkv, spatial_out, 'fpe,fqe->fpq', 'fpq,fqe->fpe')
    return sublayer(hidden, temporal_qkv, temporal_out, 'fpe,gpe->pfg', 'pfg,gpe->fpe')
```

```python
import functools
import math

import jax
import jax.numpy as jnp
from jax import lax
from jax.experimental import pallas as pl
from jax.experimental.pallas import tpu as pltpu
from jax.sharding import PartitionSpec as P

HEADS = 16
epsilon = 1e-06
MESH = pl.DeviceIdType.MESH


def normalize_into(x_ref, xt_ref, nt_ref):
    xt_ref[...] = x_ref[...].astype(jnp.float32).T
    values = xt_ref[...]
    centered = values - jnp.mean(values, axis=0, keepdims=True)
    spread = jnp.mean(centered * centered, axis=0, keepdims=True)
    nt_ref[...] = (centered * lax.rsqrt(spread + epsilon)).astype(jnp.bfloat16)


def project_shard(w_ref, shard, nt_ref, table_ref):
    blocks, rows, width = w_ref.shape[1:]
    head = table_ref.shape[1]
    out = jnp.dot(
        w_ref[shard].reshape(blocks * rows, width), nt_ref[...], preferred_element_type=jnp.float32
    ).astype(jnp.bfloat16)
    for j in range(blocks):
        table_ref[shard * blocks + j] = out[j * rows : j * rows + head]


def attend_pair(pair, table_ref, mixed_ref, same):
    head = table_ref.shape[1]
    parts = []
    for j in range(2):
        h = pair * 2 + j
        q, k, v = table_ref[h], table_ref[HEADS + h], table_ref[2 * HEADS + h]
        scores = lax.dot_general(
            k, q, (((0,), (0,)), ((), ())), preferred_element_type=jnp.float32
        ) * (1.0 / math.sqrt(head))
        if same is not None:
            scores = jnp.where(same(scores.shape), scores, -jnp.inf)
        powers = jnp.exp(scores - jnp.max(scores, axis=0, keepdims=True))
        total = jnp.sum(powers, axis=0, keepdims=True)
        probs = (powers * (1.0 / total)).astype(jnp.bfloat16)
        parts.append(jnp.dot(v, probs, preferred_element_type=jnp.float32))
    both = jnp.concatenate(parts, axis=0).astype(jnp.bfloat16)
    mixed_ref[pl.ds(pl.multiple_of(pair * 2 * head, 16), 2 * head), :] = both


def project_out(w_ref, mixed_ref, xt_ref, out_ref, head):
    shards, blocks, rows, width = w_ref.shape
    low = head // 16 * 16
    step = 4

    @pl.loop(0, shards // step)
    def _(i):
        weights = w_ref[pl.ds(i * step, step), :, low:, :].reshape(-1, width)
        update = jnp.dot(weights, mixed_ref[...], preferred_element_type=jnp.float32)
        update = update.reshape(step * blocks, rows - low, -1)[:, head - low :]
        count = step * blocks * (rows - head)
        at = pl.ds(pl.multiple_of(i * count, 8), count)
        xt_ref[at, :] = xt_ref[at, :] + update.reshape(count, -1)

    out_ref[...] = xt_ref[...].T.astype(jnp.bfloat16)


def same_by(kind, size):
    def same(shape):
        a = lax.broadcasted_iota(jnp.int32, shape, 0)
        b = lax.broadcasted_iota(jnp.int32, shape, 1)
        return (a % size == b % size) if kind == "mod" else (a // size == b // size)

    return same


def sublayer_kernel(same, x_ref, w_ref, out_ref, xt_ref, nt_ref, table_ref, mixed_ref):
    normalize_into(x_ref, xt_ref, nt_ref)

    @pl.loop(0, w_ref.shape[0])
    def _(d):
        project_shard(w_ref, d, nt_ref, table_ref)

    @pl.loop(0, HEADS // 2)
    def _(pair):
        attend_pair(pair, table_ref, mixed_ref, same)

    project_out(w_ref, mixed_ref, xt_ref, out_ref, table_ref.shape[1])


def compute_scratch(tokens, width):
    return [
        pltpu.VMEM((width, tokens), jnp.float32),
        pltpu.VMEM((width, tokens), jnp.bfloat16),
        pltpu.VMEM((3 * HEADS, width // HEADS, tokens), jnp.bfloat16),
        pltpu.VMEM((width, tokens), jnp.bfloat16),
    ]


def sublayer(x, w, same):
    tokens, width = x.shape
    return pl.pallas_call(
        functools.partial(sublayer_kernel, same),
        out_shape=jax.ShapeDtypeStruct(x.shape, jnp.bfloat16),
        in_specs=[pl.BlockSpec(memory_space=pltpu.VMEM)] * 2,
        out_specs=pl.BlockSpec(memory_space=pltpu.VMEM),
        scratch_shapes=compute_scratch(tokens, width),
        compiler_params=pltpu.CompilerParams(vmem_limit_bytes=40 << 20),
    )(x, w)


def blocks_of(qkv, out, count):
    width = qkv.shape[0]
    return jnp.concatenate(
        [qkv.T.reshape(count, -1, width), out.T.reshape(count, -1, width)], axis=1
    )


def gathered(qkv, out):
    if lax.axis_size("seq") == HEADS:
        return lax.all_gather(blocks_of(qkv, out, 3), "seq", axis=0)
    full = blocks_of(
        lax.all_gather(qkv, "seq", axis=1, tiled=True),
        lax.all_gather(out, "seq", axis=1, tiled=True),
        3 * HEADS,
    )
    return full.reshape(HEADS, 3, *full.shape[1:])


def plain(video, spatial_qkv, spatial_out, temporal_qkv, temporal_out):
    frames_here, patches, width = video.shape
    n = lax.axis_size("seq")
    count = patches // n
    same_s = None if frames_here == 1 else same_by("div", patches)
    hidden = sublayer(video.reshape(-1, width), gathered(spatial_qkv, spatial_out), same_s)
    blocks = hidden.reshape(frames_here, n, count, width)
    received = lax.all_to_all(blocks, "seq", split_axis=1, concat_axis=0, tiled=True)
    result = sublayer(
        received.reshape(-1, width), gathered(temporal_qkv, temporal_out), same_by("mod", count)
    )
    positioned = result.reshape(frames_here * n, 1, count, width)
    returned = lax.all_to_all(positioned, "seq", split_axis=0, concat_axis=1, tiled=True)
    return returned.reshape(frames_here, patches, width)


def solution(mesh):
    split = P(None, "seq")
    placed = (P(("groups", "seq"), None, None), split, split, split, split)
    return jax.shard_map(
        plain,
        mesh=mesh,
        in_specs=placed,
        out_specs=placed[0],
        check_vma=False,
    )
```

```python
import functools
import math

import jax
import jax.numpy as jnp
from jax import lax
from jax.experimental import pallas as pl
from jax.experimental.pallas import tpu as pltpu
from jax.sharding import PartitionSpec as P

HEADS = 16
epsilon = 1e-06
MESH = pl.DeviceIdType.MESH


def normalize_into(x_ref, xt_ref, nt_ref):
    xt_ref[...] = x_ref[...].astype(jnp.float32).T
    values = xt_ref[...]
    centered = values - jnp.mean(values, axis=0, keepdims=True)
    spread = jnp.mean(centered * centered, axis=0, keepdims=True)
    nt_ref[...] = (centered * lax.rsqrt(spread + epsilon)).astype(jnp.bfloat16)


def project_shard(w_ref, shard, nt_ref, table_ref):
    blocks, rows, width = w_ref.shape[1:]
    head = table_ref.shape[1]
    out = jnp.dot(
        w_ref[shard].reshape(blocks * rows, width), nt_ref[...], preferred_element_type=jnp.float32
    ).astype(jnp.bfloat16)
    for j in range(blocks):
        table_ref[shard * blocks + j] = out[j * rows : j * rows + head]


def attend_pair(pair, table_ref, mixed_ref, same):
    head = table_ref.shape[1]
    parts = []
    for j in range(2):
        h = pair * 2 + j
        q, k, v = table_ref[h], table_ref[HEADS + h], table_ref[2 * HEADS + h]
        scores = lax.dot_general(
            k, q, (((0,), (0,)), ((), ())), preferred_element_type=jnp.float32
        ) * (1.0 / math.sqrt(head))
        if same is not None:
            scores = jnp.where(same(scores.shape), scores, -jnp.inf)
        powers = jnp.exp(scores - jnp.max(scores, axis=0, keepdims=True))
        total = jnp.sum(powers, axis=0, keepdims=True)
        probs = (powers * (1.0 / total)).astype(jnp.bfloat16)
        parts.append(jnp.dot(v, probs, preferred_element_type=jnp.float32))
    both = jnp.concatenate(parts, axis=0).astype(jnp.bfloat16)
    mixed_ref[pl.ds(pl.multiple_of(pair * 2 * head, 16), 2 * head), :] = both


def project_out(w_ref, mixed_ref, xt_ref, out_ref, head):
    shards, blocks, rows, width = w_ref.shape
    low = head // 16 * 16
    step = 4

    @pl.loop(0, shards // step)
    def _(i):
        weights = w_ref[pl.ds(i * step, step), :, low:, :].reshape(-1, width)
        update = jnp.dot(weights, mixed_ref[...], preferred_element_type=jnp.float32)
        update = update.reshape(step * blocks, rows - low, -1)[:, head - low :]
        count = step * blocks * (rows - head)
        at = pl.ds(pl.multiple_of(i * count, 8), count)
        xt_ref[at, :] = xt_ref[at, :] + update.reshape(count, -1)

    out_ref[...] = xt_ref[...].T.astype(jnp.bfloat16)


def same_by(kind, size):
    def same(shape):
        a = lax.broadcasted_iota(jnp.int32, shape, 0)
        b = lax.broadcasted_iota(jnp.int32, shape, 1)
        return (a % size == b % size) if kind == "mod" else (a // size == b // size)

    return same


def sublayer_kernel(same, x_ref, w_ref, out_ref, xt_ref, nt_ref, table_ref, mixed_ref):
    normalize_into(x_ref, xt_ref, nt_ref)

    @pl.loop(0, w_ref.shape[0])
    def _(d):
        project_shard(w_ref, d, nt_ref, table_ref)

    @pl.loop(0, HEADS // 2)
    def _(pair):
        attend_pair(pair, table_ref, mixed_ref, same)

    project_out(w_ref, mixed_ref, xt_ref, out_ref, table_ref.shape[1])


def compute_scratch(tokens, width):
    return [
        pltpu.VMEM((width, tokens), jnp.float32),
        pltpu.VMEM((width, tokens), jnp.bfloat16),
        pltpu.VMEM((3 * HEADS, width // HEADS, tokens), jnp.bfloat16),
        pltpu.VMEM((width, tokens), jnp.bfloat16),
    ]


def sublayer(x, w, same):
    tokens, width = x.shape
    return pl.pallas_call(
        functools.partial(sublayer_kernel, same),
        out_shape=jax.ShapeDtypeStruct(x.shape, jnp.bfloat16),
        in_specs=[pl.BlockSpec(memory_space=pltpu.VMEM)] * 2,
        out_specs=pl.BlockSpec(memory_space=pltpu.VMEM),
        scratch_shapes=compute_scratch(tokens, width),
        compiler_params=pltpu.CompilerParams(vmem_limit_bytes=40 << 20),
    )(x, w)


def blocks_of(qkv, out, count):
    width = qkv.shape[0]
    return jnp.concatenate(
        [qkv.T.reshape(count, -1, width), out.T.reshape(count, -1, width)], axis=1
    )


def gathered(qkv, out):
    if lax.axis_size("seq") == HEADS:
        return lax.all_gather(blocks_of(qkv, out, 3), "seq", axis=0)
    full = blocks_of(
        lax.all_gather(qkv, "seq", axis=1, tiled=True),
        lax.all_gather(out, "seq", axis=1, tiled=True),
        3 * HEADS,
    )
    return full.reshape(HEADS, 3, *full.shape[1:])


def plain(video, spatial_qkv, spatial_out, temporal_qkv, temporal_out):
    frames_here, patches, width = video.shape
    n = lax.axis_size("seq")
    count = patches // n
    same_s = None if frames_here == 1 else same_by("div", patches)
    hidden = sublayer(video.reshape(-1, width), gathered(spatial_qkv, spatial_out), same_s)
    blocks = hidden.reshape(frames_here, n, count, width)
    received = lax.all_to_all(blocks, "seq", split_axis=1, concat_axis=0, tiled=True)
    result = sublayer(
        received.reshape(-1, width), gathered(temporal_qkv, temporal_out), same_by("mod", count)
    )
    positioned = result.reshape(frames_here * n, 1, count, width)
    returned = lax.all_to_all(positioned, "seq", split_axis=0, concat_axis=1, tiled=True)
    return returned.reshape(frames_here, patches, width)


def ring_position(chip, chips):
    odd = lax.rem(chip, 2)
    return (1 - odd) * lax.div(chip, 2) + odd * (chips - 1 - lax.div(chip, 2))


def ring_chip(position, chips):
    back = lax.div(position, chips // 2)
    return (1 - back) * 2 * position + back * (2 * (chips - 1 - position) + 1)


def fused_kernel(
    n, groups, count, x_ref, ws_ref, wt_ref, out_ref,
    w_ref, xt_ref, nt_ref, table_ref, mixed_ref, sent_ref, got_ref,
    land_sem, ring_sem, other_sem, sib_sem, go_sem, come_sem,
):
    chips = n // 2
    half = chips // 2
    me = lax.axis_index("seq")
    group = lax.axis_index("groups")
    core = lax.rem(me, 2)
    sibling = me + 1 - 2 * core
    side = lax.rem(group, 2)
    other = group + 1 - 2 * side
    place = ring_position(lax.div(me, 2), chips)
    by_ring, by_other = 2 * side, 2 - 2 * side

    def device(offset, which):
        return 2 * ring_chip(lax.rem(place + offset + chips, chips), chips) + which

    ahead = (device(1, core), device(-1, core))

    barrier = pltpu.get_barrier_semaphore()
    for j in range(1, n):
        pl.semaphore_signal(
            barrier, inc=1, device_id={"seq": lax.rem(me + j, n)}, device_id_type=MESH
        )
    pl.semaphore_signal(barrier, inc=1, device_id={"groups": other}, device_id_type=MESH)
    pl.semaphore_wait(barrier, n)

    sends = []

    def copy(phase, shard, piece, send_sem, target):
        return pltpu.make_async_remote_copy(
            src_ref=w_ref.at[phase, shard, piece],
            dst_ref=w_ref.at[phase, shard, piece],
            send_sem=send_sem.at[phase, shard, piece],
            recv_sem=land_sem.at[phase, shard, piece],
            device_id=target,
            device_id_type=MESH,
        )

    def send(*what):
        one = copy(*what)
        one.start()
        sends.append(one)

    def along(phase, shard, piece, way):
        send(phase, shard, piece, ring_sem.at[way], {"seq": ahead[way]})

    def beside(phase, shard, piece):
        send(phase, shard, piece, sib_sem, {"seq": sibling})

    def across(phase, shard):
        send(phase, shard, by_ring, other_sem, {"groups": other})

    def landed(phase, shard, piece):
        copy(phase, shard, piece, sib_sem, {"seq": sibling}).wait_recv()

    reach = ((by_ring, (half - 1, half)), (1, (half, half - 1)))

    def start(phase):
        for piece, far in reach:
            for way in range(2):
                along(phase, me, piece, way)
        for piece in range(3):
            beside(phase, me, piece)

    def step(phase, s):
        for piece, far in reach:
            for way in range(2):
                if s <= far[way]:
                    shard = device(-s if way == 0 else s, core)
                    landed(phase, shard, piece)
                    if s < far[way]:
                        along(phase, shard, piece, way)
                    if piece is by_ring:
                        across(phase, shard)
                    beside(phase, shard, piece)

    def offsets(s):
        return (0,) if s == 0 else (s,) if s == half else (-s, s)

    def from_other(phase, s):
        for offset in offsets(s):
            shard = device(offset, core)
            landed(phase, shard, by_other)
            beside(phase, shard, by_other)

    def from_sibling(phase, s):
        for offset in offsets(s):
            for piece in range(3):
                landed(phase, device(offset, 1 - core), piece)

    def project(phase, s, which):
        for offset in offsets(s):
            project_shard(w_ref.at[phase], device(offset, which), nt_ref, table_ref)

    def rows(index):
        return pl.ds(pl.multiple_of(index * count, count), count)

    def swap(phase, away, home):
        return pltpu.make_async_remote_copy(
            src_ref=sent_ref.at[phase, rows(away), :],
            dst_ref=got_ref.at[phase, rows(home), :],
            send_sem=go_sem.at[phase, away],
            recv_sem=come_sem.at[phase, home],
            device_id={"seq": away},
            device_id_type=MESH,
        )

    def exchange(phase):
        for j in range(1, n):
            one = swap(phase, lax.rem(me + j, n), me)
            one.start()
            sends.append(one)
        got_ref[phase, rows(me), :] = sent_ref[phase, rows(me), :]

    def exchanged(phase):
        for j in range(1, n):
            peer = lax.rem(me + j, n)
            swap(phase, peer, peer).wait_recv()

    def attend(low, high, same):
        @pl.loop(low, high)
        def _(pair):
            attend_pair(pair, table_ref, mixed_ref, same)

    head = table_ref.shape[1]
    pairs = HEADS // 2

    w_ref[0, me] = ws_ref[...]
    start(0)
    w_ref[1, me] = wt_ref[...]
    normalize_into(x_ref, xt_ref, nt_ref)
    project(0, 0, core)
    for s in range(1, half + 1):
        step(0, s)
        if s == half - 1:
            start(1)
        if s > 1:
            from_other(0, s - 1)
            project(0, s - 1, core)
        from_sibling(0, max(s - 2, 0)) if s != 2 else None
        project(0, max(s - 2, 0), 1 - core) if s != 2 else None
    from_other(0, half)
    project(0, half, core)
    step(1, 1)
    for s in range(half - 1, half + 1):
        from_sibling(0, s)
        project(0, s, 1 - core)
    attend(0, pairs, None)
    step(1, 2)
    project_out(w_ref.at[0], mixed_ref, xt_ref, sent_ref.at[0], head)
    exchange(0)
    from_other(1, 1)
    for s in range(3, half + 1):
        step(1, s)
        from_other(1, s - 1)
    exchanged(0)
    normalize_into(got_ref.at[0], xt_ref, nt_ref)
    project(1, 0, core)
    from_sibling(1, 0)
    project(1, 0, 1 - core)
    from_other(1, half)
    for s in range(1, half + 1):
        project(1, s, core)
    for s in range(1, half + 1):
        from_sibling(1, s)
        project(1, s, 1 - core)
    attend(0, pairs, same_by("mod", count))
    project_out(w_ref.at[1], mixed_ref, xt_ref, sent_ref.at[1], head)
    exchange(1)
    exchanged(1)
    out_ref[...] = got_ref[1]
    for one in sends:
        one.wait_send()


def fused(video, spatial_qkv, spatial_out, temporal_qkv, temporal_out):
    _, patches, width = video.shape
    n, groups = lax.axis_size("seq"), lax.axis_size("groups")
    ws = blocks_of(spatial_qkv, spatial_out, 3)
    wt = blocks_of(temporal_qkv, temporal_out, 3)
    dma = pltpu.SemaphoreType.DMA
    out = pl.pallas_call(
        functools.partial(fused_kernel, n, groups, patches // n),
        out_shape=jax.ShapeDtypeStruct((patches, width), jnp.bfloat16),
        in_specs=[pl.BlockSpec(memory_space=pltpu.VMEM)] * 3,
        out_specs=pl.BlockSpec(memory_space=pltpu.VMEM),
        scratch_shapes=[pltpu.VMEM((2, n, *ws.shape), jnp.bfloat16)]
        + compute_scratch(patches, width)
        + [pltpu.VMEM((2, patches, width), jnp.bfloat16)] * 2
        + [dma((2, n, 3)), dma((2, 2, n, 3)), dma((2, n, 3)), dma((2, n, 3))]
        + [dma((2, n)), dma((2, n))],
        compiler_params=pltpu.CompilerParams(
            collective_id=0, has_side_effects=True, vmem_limit_bytes=56 << 20
        ),
    )(video.reshape(patches, width), ws, wt)
    return out.reshape(video.shape)


def local(video, spatial_qkv, *rest):
    n, groups = lax.axis_size("seq"), lax.axis_size("groups")
    frames_here, patches, _ = video.shape
    ringed = n == HEADS and groups % 2 == 0 and frames_here == 1 and patches % (16 * n) == 0
    return (fused if ringed else plain)(video, spatial_qkv, *rest)


def solution(mesh):
    split = P(None, "seq")
    placed = (P(("groups", "seq"), None, None), split, split, split, split)
    return jax.shard_map(
        local,
        mesh=mesh,
        in_specs=placed,
        out_specs=placed[0],
        check_vma=False,
    )
```

```python
import functools
import math

import jax
import jax.numpy as jnp
from jax import lax
from jax.experimental import pallas as pl
from jax.experimental.pallas import tpu as pltpu
from jax.sharding import PartitionSpec as P

HEADS = 16
epsilon = 1e-06
MESH = pl.DeviceIdType.MESH


def normalize_into(x_ref, xt_ref, nt_ref):
    xt_ref[...] = x_ref[...].astype(jnp.float32).T
    values = xt_ref[...]
    centered = values - jnp.mean(values, axis=0, keepdims=True)
    spread = jnp.mean(centered * centered, axis=0, keepdims=True)
    nt_ref[...] = (centered * lax.rsqrt(spread + epsilon)).astype(jnp.bfloat16)


def project_shard(w_ref, shard, nt_ref, table_ref):
    blocks, rows, width = w_ref.shape[1:]
    head = table_ref.shape[1]
    out = jnp.dot(
        w_ref[shard].reshape(blocks * rows, width), nt_ref[...], preferred_element_type=jnp.float32
    ).astype(jnp.bfloat16)
    for j in range(blocks):
        table_ref[shard * blocks + j] = out[j * rows : j * rows + head]


def attend_pair(pair, table_ref, mixed_ref, same, low=0, high=None):
    head = table_ref.shape[1]
    parts = []
    for j in range(2):
        h = pair * 2 + j
        q, k, v = table_ref[h, :, low:high], table_ref[HEADS + h], table_ref[2 * HEADS + h]
        scores = lax.dot_general(
            k, q, (((0,), (0,)), ((), ())), preferred_element_type=jnp.float32
        ) * (1.0 / math.sqrt(head))
        if same is not None:
            scores = jnp.where(same(scores.shape), scores, -jnp.inf)
        powers = jnp.exp(scores - jnp.max(scores, axis=0, keepdims=True))
        total = jnp.sum(powers, axis=0, keepdims=True)
        probs = (powers * (1.0 / total)).astype(jnp.bfloat16)
        parts.append(jnp.dot(v, probs, preferred_element_type=jnp.float32))
    both = jnp.concatenate(parts, axis=0).astype(jnp.bfloat16)
    mixed_ref[pl.ds(pl.multiple_of(pair * 2 * head, 16), 2 * head), low:high] = both


def project_out(w_ref, mixed_ref, xt_ref, out_ref, head, first=0, last=None):
    shards, blocks, rows, width = w_ref.shape
    low = head // 16 * 16
    step = 4
    tokens = slice(first, last)

    @pl.loop(0, shards // step)
    def _(i):
        weights = w_ref[pl.ds(i * step, step), :, low:, :].reshape(-1, width)
        update = jnp.dot(weights, mixed_ref[:, tokens], preferred_element_type=jnp.float32)
        update = update.reshape(step * blocks, rows - low, -1)[:, head - low :]
        count = step * blocks * (rows - head)
        at = pl.ds(pl.multiple_of(i * count, 8), count)
        xt_ref[at, tokens] = xt_ref[at, tokens] + update.reshape(count, -1)

    out_ref[tokens, :] = xt_ref[:, tokens].T.astype(jnp.bfloat16)


def same_by(kind, size):
    def same(shape):
        a = lax.broadcasted_iota(jnp.int32, shape, 0)
        b = lax.broadcasted_iota(jnp.int32, shape, 1)
        return (a % size == b % size) if kind == "mod" else (a // size == b // size)

    return same


def sublayer_kernel(same, x_ref, w_ref, out_ref, xt_ref, nt_ref, table_ref, mixed_ref):
    normalize_into(x_ref, xt_ref, nt_ref)

    @pl.loop(0, w_ref.shape[0])
    def _(d):
        project_shard(w_ref, d, nt_ref, table_ref)

    @pl.loop(0, HEADS // 2)
    def _(pair):
        attend_pair(pair, table_ref, mixed_ref, same)

    project_out(w_ref, mixed_ref, xt_ref, out_ref, table_ref.shape[1])


def compute_scratch(tokens, width):
    return [
        pltpu.VMEM((width, tokens), jnp.float32),
        pltpu.VMEM((width, tokens), jnp.bfloat16),
        pltpu.VMEM((3 * HEADS, width // HEADS, tokens), jnp.bfloat16),
        pltpu.VMEM((width, tokens), jnp.bfloat16),
    ]


def sublayer(x, w, same):
    tokens, width = x.shape
    return pl.pallas_call(
        functools.partial(sublayer_kernel, same),
        out_shape=jax.ShapeDtypeStruct(x.shape, jnp.bfloat16),
        in_specs=[pl.BlockSpec(memory_space=pltpu.VMEM)] * 2,
        out_specs=pl.BlockSpec(memory_space=pltpu.VMEM),
        scratch_shapes=compute_scratch(tokens, width),
        compiler_params=pltpu.CompilerParams(vmem_limit_bytes=40 << 20),
    )(x, w)


def blocks_of(qkv, out, count):
    width = qkv.shape[0]
    return jnp.concatenate(
        [qkv.T.reshape(count, -1, width), out.T.reshape(count, -1, width)], axis=1
    )


def gathered(qkv, out):
    if lax.axis_size("seq") == HEADS:
        return lax.all_gather(blocks_of(qkv, out, 3), "seq", axis=0)
    full = blocks_of(
        lax.all_gather(qkv, "seq", axis=1, tiled=True),
        lax.all_gather(out, "seq", axis=1, tiled=True),
        3 * HEADS,
    )
    return full.reshape(HEADS, 3, *full.shape[1:])


def plain(video, spatial_qkv, spatial_out, temporal_qkv, temporal_out):
    frames_here, patches, width = video.shape
    n = lax.axis_size("seq")
    count = patches // n
    same_s = None if frames_here == 1 else same_by("div", patches)
    hidden = sublayer(video.reshape(-1, width), gathered(spatial_qkv, spatial_out), same_s)
    blocks = hidden.reshape(frames_here, n, count, width)
    received = lax.all_to_all(blocks, "seq", split_axis=1, concat_axis=0, tiled=True)
    result = sublayer(
        received.reshape(-1, width), gathered(temporal_qkv, temporal_out), same_by("mod", count)
    )
    positioned = result.reshape(frames_here * n, 1, count, width)
    returned = lax.all_to_all(positioned, "seq", split_axis=0, concat_axis=1, tiled=True)
    return returned.reshape(frames_here, patches, width)


def ring_position(chip, chips):
    odd = lax.rem(chip, 2)
    return (1 - odd) * lax.div(chip, 2) + odd * (chips - 1 - lax.div(chip, 2))


def ring_chip(position, chips):
    back = lax.div(position, chips // 2)
    return (1 - back) * 2 * position + back * (2 * (chips - 1 - position) + 1)


def fused_kernel(
    n, groups, count, x_ref, ws_ref, wt_ref, out_ref,
    w_ref, xt_ref, nt_ref, table_ref, mixed_ref, sent_ref, got_ref,
    land_sem, ring_sem, other_sem, sib_sem, go_sem, come_sem,
):
    chips = n // 2
    half = chips // 2
    me = lax.axis_index("seq")
    group = lax.axis_index("groups")
    core = lax.rem(me, 2)
    sibling = me + 1 - 2 * core
    side = lax.rem(group, 2)
    other = group + 1 - 2 * side
    place = ring_position(lax.div(me, 2), chips)
    by_ring, by_other = 2 * side, 2 - 2 * side

    def device(offset, which):
        return 2 * ring_chip(lax.rem(place + offset + chips, chips), chips) + which

    ahead = (device(1, core), device(-1, core))

    barrier = pltpu.get_barrier_semaphore()
    for j in range(1, n):
        pl.semaphore_signal(
            barrier, inc=1, device_id={"seq": lax.rem(me + j, n)}, device_id_type=MESH
        )
    pl.semaphore_signal(barrier, inc=1, device_id={"groups": other}, device_id_type=MESH)
    pl.semaphore_wait(barrier, n)

    sends = []

    def copy(phase, shard, piece, send_sem, target):
        return pltpu.make_async_remote_copy(
            src_ref=w_ref.at[phase, shard, piece],
            dst_ref=w_ref.at[phase, shard, piece],
            send_sem=send_sem.at[phase, shard, piece],
            recv_sem=land_sem.at[phase, shard, piece],
            device_id=target,
            device_id_type=MESH,
        )

    def send(*what):
        one = copy(*what)
        one.start()
        sends.append(one)

    def along(phase, shard, piece, way):
        send(phase, shard, piece, ring_sem.at[way], {"seq": ahead[way]})

    def whole(phase, shard):
        return pltpu.make_async_remote_copy(
            src_ref=w_ref.at[phase, shard],
            dst_ref=w_ref.at[phase, shard],
            send_sem=sib_sem.at[phase, shard],
            recv_sem=land_sem.at[phase, shard, 0],
            device_id={"seq": sibling},
            device_id_type=MESH,
        )

    def beside(phase, shard):
        one = whole(phase, shard)
        one.start()
        sends.append(one)

    def across(phase, shard):
        send(phase, shard, by_ring, other_sem, {"groups": other})

    def landed(phase, shard, piece):
        copy(phase, shard, piece, other_sem, {"groups": other}).wait_recv()

    reach = ((by_ring, (half - 1, half)), (1, (half, half - 1)))

    def start(phase):
        for piece, far in reach:
            for way in range(2):
                along(phase, me, piece, way)
        beside(phase, me)

    def step(phase, s):
        for piece, far in reach:
            for way in range(2):
                if s <= far[way]:
                    shard = device(-s if way == 0 else s, core)
                    landed(phase, shard, piece)
                    if s < far[way]:
                        along(phase, shard, piece, way)
                    if piece is by_ring:
                        across(phase, shard)

    def offsets(s):
        return (0,) if s == 0 else (s,) if s == half else (-s, s)

    def from_other(phase, s):
        for offset in offsets(s):
            shard = device(offset, core)
            landed(phase, shard, by_other)
            beside(phase, shard)

    def from_sibling(phase, s):
        for offset in offsets(s):
            whole(phase, device(offset, 1 - core)).wait_recv()

    def project(phase, s, which):
        for offset in offsets(s):
            project_shard(w_ref.at[phase], device(offset, which), nt_ref, table_ref)

    def rows(index):
        return pl.ds(pl.multiple_of(index * count, count), count)

    def slot(index):
        return lax.rem(index, 2) * chips + lax.div(index, 2)

    def swap(phase, away, home):
        leaving = rows(away if phase == 0 else slot(away))
        landing = rows(slot(home) if phase == 0 else home)
        return pltpu.make_async_remote_copy(
            src_ref=sent_ref.at[phase, leaving, :],
            dst_ref=got_ref.at[phase, landing, :],
            send_sem=go_sem.at[phase, away],
            recv_sem=come_sem.at[phase, home],
            device_id={"seq": away},
            device_id_type=MESH,
        )

    def exchange(phase, start=True):
        for j in range(1, n):
            one = swap(phase, lax.rem(me + j, n), me)
            if start:
                one.start()
            sends.append(one)

    def exchange_half(which):
        for j in range(chips):
            away = 2 * lax.rem(lax.div(me, 2) + j, chips) + which
            if j == 0:

                @pl.when(core != which)
                def _():
                    swap(1, away, me).start()

            else:
                swap(1, away, me).start()

    def exchanged(phase):
        for j in range(1, n):
            peer = lax.rem(me + j, n)
            swap(phase, peer, peer).wait_recv()

    def attend(low, high, same, *tokens):
        @pl.loop(low, high)
        def _(pair):
            attend_pair(pair, table_ref, mixed_ref, same, *tokens)

    head = table_ref.shape[1]
    pairs = HEADS // 2

    w_ref[0, me] = ws_ref[...]
    start(0)
    w_ref[1, me] = wt_ref[...]
    normalize_into(x_ref, xt_ref, nt_ref)
    project(0, 0, core)
    for s in range(1, half + 1):
        step(0, s)
        if s == half - 1:
            start(1)
        if s > 1:
            from_other(0, s - 1)
            project(0, s - 1, core)
        from_sibling(0, max(s - 2, 0)) if s != 2 else None
        project(0, max(s - 2, 0), 1 - core) if s != 2 else None
    from_other(0, half)
    project(0, half, core)
    step(1, 1)
    for s in range(half - 1, half + 1):
        from_sibling(0, s)
        project(0, s, 1 - core)
    attend(0, pairs, None)
    step(1, 2)
    project_out(w_ref.at[0], mixed_ref, xt_ref, sent_ref.at[0], head)
    exchange(0)
    got_ref[0, rows(slot(me)), :] = sent_ref[0, rows(me), :]
    from_other(1, 1)
    for s in range(3, half + 1):
        step(1, s)
        from_other(1, s - 1)
    exchanged(0)
    normalize_into(got_ref.at[0], xt_ref, nt_ref)
    project(1, 0, core)
    from_sibling(1, 0)
    project(1, 0, 1 - core)
    for s in range(1, half):
        project(1, s, core)
    from_other(1, half)
    project(1, half, core)
    for s in range(1, half + 1):
        from_sibling(1, s)
        project(1, s, 1 - core)
    for which in range(2):
        tokens = (which * chips * count, (which + 1) * chips * count)
        attend(0, pairs, same_by("mod", count), *tokens)
        project_out(w_ref.at[1], mixed_ref, xt_ref, sent_ref.at[1], head, *tokens)
        exchange_half(which)
    exchange(1, start=False)
    got_ref[1, rows(me), :] = sent_ref[1, rows(slot(me)), :]
    exchanged(1)
    out_ref[...] = got_ref[1]
    for one in sends:
        one.wait_send()


def fused(video, spatial_qkv, spatial_out, temporal_qkv, temporal_out):
    _, patches, width = video.shape
    n, groups = lax.axis_size("seq"), lax.axis_size("groups")
    ws = blocks_of(spatial_qkv, spatial_out, 3)
    wt = blocks_of(temporal_qkv, temporal_out, 3)
    dma = pltpu.SemaphoreType.DMA
    out = pl.pallas_call(
        functools.partial(fused_kernel, n, groups, patches // n),
        out_shape=jax.ShapeDtypeStruct((patches, width), jnp.bfloat16),
        in_specs=[pl.BlockSpec(memory_space=pltpu.VMEM)] * 3,
        out_specs=pl.BlockSpec(memory_space=pltpu.VMEM),
        scratch_shapes=[pltpu.VMEM((2, n, *ws.shape), jnp.bfloat16)]
        + compute_scratch(patches, width)
        + [pltpu.VMEM((2, patches, width), jnp.bfloat16)] * 2
        + [dma((2, n, 3)), dma((2, 2, n, 3)), dma((2, n, 3)), dma((2, n))]
        + [dma((2, n)), dma((2, n))],
        compiler_params=pltpu.CompilerParams(
            collective_id=0, has_side_effects=True, vmem_limit_bytes=56 << 20
        ),
    )(video.reshape(patches, width), ws, wt)
    return out.reshape(video.shape)


def local(video, spatial_qkv, *rest):
    n, groups = lax.axis_size("seq"), lax.axis_size("groups")
    frames_here, patches, _ = video.shape
    ringed = n == HEADS and groups % 2 == 0 and frames_here == 1 and patches % (16 * n) == 0
    return (fused if ringed else plain)(video, spatial_qkv, *rest)


def solution(mesh):
    split = P(None, "seq")
    placed = (P(("groups", "seq"), None, None), split, split, split, split)
    return jax.shard_map(
        local,
        mesh=mesh,
        in_specs=placed,
        out_specs=placed[0],
        check_vma=False,
    )
```

```python
import functools
import math

import jax
import jax.numpy as jnp
from jax import lax
from jax.experimental import pallas as pl
from jax.experimental.pallas import tpu as pltpu
from jax.sharding import PartitionSpec as P

HEADS = 16
epsilon = 1e-06
MESH = pl.DeviceIdType.MESH


def normalize_into(x_ref, xt_ref, nt_ref):
    xt_ref[...] = x_ref[...].astype(jnp.float32).T
    values = xt_ref[...]
    centered = values - jnp.mean(values, axis=0, keepdims=True)
    spread = jnp.mean(centered * centered, axis=0, keepdims=True)
    nt_ref[...] = (centered * lax.rsqrt(spread + epsilon)).astype(jnp.bfloat16)


def project_shard(w_ref, shard, nt_ref, table_ref):
    blocks, rows, width = w_ref.shape[1:]
    head = table_ref.shape[1]
    out = jnp.dot(
        w_ref[shard].reshape(blocks * rows, width), nt_ref[...], preferred_element_type=jnp.float32
    ).astype(jnp.bfloat16)
    for j in range(blocks):
        table_ref[shard * blocks + j] = out[j * rows : j * rows + head]


def attend_pair(pair, table_ref, mixed_ref, same, low=0, high=None):
    head = table_ref.shape[1]
    parts = []
    for j in range(2):
        h = pair * 2 + j
        q, k, v = table_ref[h, :, low:high], table_ref[HEADS + h], table_ref[2 * HEADS + h]
        scores = lax.dot_general(
            k, q, (((0,), (0,)), ((), ())), preferred_element_type=jnp.float32
        ) * (1.0 / math.sqrt(head))
        if same is not None:
            scores = jnp.where(same(scores.shape), scores, -jnp.inf)
        powers = jnp.exp(scores - jnp.max(scores, axis=0, keepdims=True))
        total = jnp.sum(powers, axis=0, keepdims=True)
        probs = (powers * (1.0 / total)).astype(jnp.bfloat16)
        parts.append(jnp.dot(v, probs, preferred_element_type=jnp.float32))
    both = jnp.concatenate(parts, axis=0).astype(jnp.bfloat16)
    mixed_ref[pl.ds(pl.multiple_of(pair * 2 * head, 16), 2 * head), low:high] = both


def project_out(w_ref, mixed_ref, xt_ref, out_ref, head, first=0, last=None):
    shards, blocks, rows, width = w_ref.shape
    low = head // 16 * 16
    step = 4
    tokens = slice(first, last)

    @pl.loop(0, shards // step)
    def _(i):
        weights = w_ref[pl.ds(i * step, step), :, low:, :].reshape(-1, width)
        update = jnp.dot(weights, mixed_ref[:, tokens], preferred_element_type=jnp.float32)
        update = update.reshape(step * blocks, rows - low, -1)[:, head - low :]
        count = step * blocks * (rows - head)
        at = pl.ds(pl.multiple_of(i * count, 8), count)
        xt_ref[at, tokens] = xt_ref[at, tokens] + update.reshape(count, -1)

    out_ref[tokens, :] = xt_ref[:, tokens].T.astype(jnp.bfloat16)


def same_by(kind, size):
    def same(shape):
        a = lax.broadcasted_iota(jnp.int32, shape, 0)
        b = lax.broadcasted_iota(jnp.int32, shape, 1)
        return (a % size == b % size) if kind == "mod" else (a // size == b // size)

    return same


def sublayer_kernel(same, x_ref, w_ref, out_ref, xt_ref, nt_ref, table_ref, mixed_ref):
    normalize_into(x_ref, xt_ref, nt_ref)

    @pl.loop(0, w_ref.shape[0])
    def _(d):
        project_shard(w_ref, d, nt_ref, table_ref)

    @pl.loop(0, HEADS // 2)
    def _(pair):
        attend_pair(pair, table_ref, mixed_ref, same)

    project_out(w_ref, mixed_ref, xt_ref, out_ref, table_ref.shape[1])


def compute_scratch(tokens, width):
    return [
        pltpu.VMEM((width, tokens), jnp.float32),
        pltpu.VMEM((width, tokens), jnp.bfloat16),
        pltpu.VMEM((3 * HEADS, width // HEADS, tokens), jnp.bfloat16),
        pltpu.VMEM((width, tokens), jnp.bfloat16),
    ]


def sublayer(x, w, same):
    tokens, width = x.shape
    return pl.pallas_call(
        functools.partial(sublayer_kernel, same),
        out_shape=jax.ShapeDtypeStruct(x.shape, jnp.bfloat16),
        in_specs=[pl.BlockSpec(memory_space=pltpu.VMEM)] * 2,
        out_specs=pl.BlockSpec(memory_space=pltpu.VMEM),
        scratch_shapes=compute_scratch(tokens, width),
        compiler_params=pltpu.CompilerParams(vmem_limit_bytes=40 << 20),
    )(x, w)


def blocks_of(qkv, out, count):
    width = qkv.shape[0]
    return jnp.concatenate(
        [qkv.T.reshape(count, -1, width), out.T.reshape(count, -1, width)], axis=1
    )


def gathered(qkv, out):
    if lax.axis_size("seq") == HEADS:
        return lax.all_gather(blocks_of(qkv, out, 3), "seq", axis=0)
    full = blocks_of(
        lax.all_gather(qkv, "seq", axis=1, tiled=True),
        lax.all_gather(out, "seq", axis=1, tiled=True),
        3 * HEADS,
    )
    return full.reshape(HEADS, 3, *full.shape[1:])


def plain(video, spatial_qkv, spatial_out, temporal_qkv, temporal_out):
    frames_here, patches, width = video.shape
    n = lax.axis_size("seq")
    count = patches // n
    same_s = None if frames_here == 1 else same_by("div", patches)
    hidden = sublayer(video.reshape(-1, width), gathered(spatial_qkv, spatial_out), same_s)
    blocks = hidden.reshape(frames_here, n, count, width)
    received = lax.all_to_all(blocks, "seq", split_axis=1, concat_axis=0, tiled=True)
    result = sublayer(
        received.reshape(-1, width), gathered(temporal_qkv, temporal_out), same_by("mod", count)
    )
    positioned = result.reshape(frames_here * n, 1, count, width)
    returned = lax.all_to_all(positioned, "seq", split_axis=0, concat_axis=1, tiled=True)
    return returned.reshape(frames_here, patches, width)


def ring_position(chip, chips):
    odd = lax.rem(chip, 2)
    return (1 - odd) * lax.div(chip, 2) + odd * (chips - 1 - lax.div(chip, 2))


def ring_chip(position, chips):
    back = lax.div(position, chips // 2)
    return (1 - back) * 2 * position + back * (2 * (chips - 1 - position) + 1)


def fused_kernel(
    n, groups, count, x_ref, ws_ref, wt_ref, out_ref,
    w_ref, xt_ref, nt_ref, table_ref, mixed_ref, sent_ref, got_ref,
    land_sem, ring_sem, other_sem, sib_sem, go_sem, come_sem,
):
    chips = n // 2
    half = chips // 2
    me = lax.axis_index("seq")
    group = lax.axis_index("groups")
    core = lax.rem(me, 2)
    sibling = me + 1 - 2 * core
    side = lax.rem(group, 2)
    other = group + 1 - 2 * side
    place = ring_position(lax.div(me, 2), chips)
    by_ring, by_other = 2 * side, 2 - 2 * side

    def device(offset, which):
        return 2 * ring_chip(lax.rem(place + offset + chips, chips), chips) + which

    ahead = (device(1, core), device(-1, core))

    barrier = pltpu.get_barrier_semaphore()
    for j in range(1, n):
        pl.semaphore_signal(
            barrier, inc=1, device_id={"seq": lax.rem(me + j, n)}, device_id_type=MESH
        )
    pl.semaphore_signal(barrier, inc=1, device_id={"groups": other}, device_id_type=MESH)
    pl.semaphore_wait(barrier, n)

    sends = []

    def copy(phase, shard, piece, send_sem, target):
        return pltpu.make_async_remote_copy(
            src_ref=w_ref.at[phase, shard, piece],
            dst_ref=w_ref.at[phase, shard, piece],
            send_sem=send_sem.at[phase, shard, piece],
            recv_sem=land_sem.at[phase, shard, piece],
            device_id=target,
            device_id_type=MESH,
        )

    def send(*what):
        one = copy(*what)
        one.start()
        sends.append(one)

    def along(phase, shard, piece, way):
        send(phase, shard, piece, ring_sem.at[way], {"seq": ahead[way]})

    def whole(phase, shard):
        return pltpu.make_async_remote_copy(
            src_ref=w_ref.at[phase, shard],
            dst_ref=w_ref.at[phase, shard],
            send_sem=sib_sem.at[phase, shard],
            recv_sem=land_sem.at[phase, shard, 0],
            device_id={"seq": sibling},
            device_id_type=MESH,
        )

    def beside(phase, shard):
        one = whole(phase, shard)
        one.start()
        sends.append(one)

    def across(phase, shard):
        send(phase, shard, by_ring, other_sem, {"groups": other})

    def landed(phase, shard, piece):
        copy(phase, shard, piece, other_sem, {"groups": other}).wait_recv()

    reach = ((by_ring, (half - 1, half)), (1, (half, half - 1)))

    def start(phase):
        for piece, far in reach:
            for way in range(2):
                along(phase, me, piece, way)
        beside(phase, me)

    def step(phase, s):
        for piece, far in reach:
            for way in range(2):
                if s <= far[way]:
                    shard = device(-s if way == 0 else s, core)
                    landed(phase, shard, piece)
                    if s < far[way]:
                        along(phase, shard, piece, way)
                    if piece is by_ring:
                        across(phase, shard)

    def offsets(s):
        return (0,) if s == 0 else (s,) if s == half else (-s, s)

    def from_other(phase, s):
        for offset in offsets(s):
            shard = device(offset, core)
            landed(phase, shard, by_other)
            beside(phase, shard)

    def from_sibling(phase, s):
        for offset in offsets(s):
            whole(phase, device(offset, 1 - core)).wait_recv()

    def project(phase, s, which):
        for offset in offsets(s):
            project_shard(w_ref.at[phase], device(offset, which), nt_ref, table_ref)

    def rows(index):
        return pl.ds(pl.multiple_of(index * count, count), count)

    def slot(index):
        return lax.rem(index, 2) * chips + lax.div(index, 2)

    def swap(phase, away, home):
        leaving = rows(away if phase == 0 else slot(away))
        landing = rows(slot(home) if phase == 0 else home)
        return pltpu.make_async_remote_copy(
            src_ref=sent_ref.at[phase, leaving, :],
            dst_ref=got_ref.at[phase, landing, :],
            send_sem=go_sem.at[phase, away],
            recv_sem=come_sem.at[phase, home],
            device_id={"seq": away},
            device_id_type=MESH,
        )

    def exchange(phase, start=True):
        for j in sorted(range(1, n), key=lambda i: -min(i, n - i)):
            one = swap(phase, lax.rem(me + j, n), me)
            if start:
                one.start()
            sends.append(one)

    def exchange_half(which):
        for j in range(chips):
            away = 2 * lax.rem(lax.div(me, 2) + j, chips) + which
            if j == 0:

                @pl.when(core != which)
                def _():
                    swap(1, away, me).start()

            else:
                swap(1, away, me).start()

    def exchanged(phase):
        for j in range(1, n):
            peer = lax.rem(me + j, n)
            swap(phase, peer, peer).wait_recv()

    def attend(low, high, same, *tokens):
        @pl.loop(low, high)
        def _(pair):
            attend_pair(pair, table_ref, mixed_ref, same, *tokens)

    head = table_ref.shape[1]
    pairs = HEADS // 2

    w_ref[0, me] = ws_ref[...]
    start(0)
    w_ref[1, me] = wt_ref[...]
    normalize_into(x_ref, xt_ref, nt_ref)
    project(0, 0, core)
    for s in range(1, half + 1):
        step(0, s)
        if s == half - 1:
            start(1)
        if s > 1:
            from_other(0, s - 1)
            project(0, s - 1, core)
        from_sibling(0, s - 1)
        project(0, s - 1, 1 - core)
    from_other(0, half)
    project(0, half, core)
    step(1, 1)
    from_sibling(0, half)
    project(0, half, 1 - core)
    attend(0, pairs, None)
    step(1, 2)
    project_out(w_ref.at[0], mixed_ref, xt_ref, sent_ref.at[0], head)
    exchange(0)
    got_ref[0, rows(slot(me)), :] = sent_ref[0, rows(me), :]
    from_other(1, 1)
    for s in range(3, half + 1):
        step(1, s)
        from_other(1, s - 1)
    exchanged(0)
    normalize_into(got_ref.at[0], xt_ref, nt_ref)
    project(1, 0, core)
    from_sibling(1, 0)
    project(1, 0, 1 - core)
    for s in range(1, half):
        project(1, s, core)
    from_other(1, half)
    project(1, half, core)
    for s in range(1, half + 1):
        from_sibling(1, s)
        project(1, s, 1 - core)
    for which in range(2):
        tokens = (which * chips * count, (which + 1) * chips * count)
        attend(0, pairs, same_by("mod", count), *tokens)
        project_out(w_ref.at[1], mixed_ref, xt_ref, sent_ref.at[1], head, *tokens)
        exchange_half(which)
    exchange(1, start=False)
    got_ref[1, rows(me), :] = sent_ref[1, rows(slot(me)), :]
    exchanged(1)
    out_ref[...] = got_ref[1]
    for one in sends:
        one.wait_send()


def fused(video, spatial_qkv, spatial_out, temporal_qkv, temporal_out):
    _, patches, width = video.shape
    n, groups = lax.axis_size("seq"), lax.axis_size("groups")
    ws = blocks_of(spatial_qkv, spatial_out, 3)
    wt = blocks_of(temporal_qkv, temporal_out, 3)
    dma = pltpu.SemaphoreType.DMA
    out = pl.pallas_call(
        functools.partial(fused_kernel, n, groups, patches // n),
        out_shape=jax.ShapeDtypeStruct((patches, width), jnp.bfloat16),
        in_specs=[pl.BlockSpec(memory_space=pltpu.VMEM)] * 3,
        out_specs=pl.BlockSpec(memory_space=pltpu.VMEM),
        scratch_shapes=[pltpu.VMEM((2, n, *ws.shape), jnp.bfloat16)]
        + compute_scratch(patches, width)
        + [pltpu.VMEM((2, patches, width), jnp.bfloat16)] * 2
        + [dma((2, n, 3)), dma((2, 2, n, 3)), dma((2, n, 3)), dma((2, n))]
        + [dma((2, n)), dma((2, n))],
        compiler_params=pltpu.CompilerParams(
            collective_id=0, has_side_effects=True, vmem_limit_bytes=56 << 20
        ),
    )(video.reshape(patches, width), ws, wt)
    return out.reshape(video.shape)


def local(video, spatial_qkv, *rest):
    n, groups = lax.axis_size("seq"), lax.axis_size("groups")
    frames_here, patches, _ = video.shape
    ringed = n == HEADS and groups % 2 == 0 and frames_here == 1 and patches % (16 * n) == 0
    return (fused if ringed else plain)(video, spatial_qkv, *rest)


def solution(mesh):
    split = P(None, "seq")
    placed = (P(("groups", "seq"), None, None), split, split, split, split)
    return jax.shard_map(
        local,
        mesh=mesh,
        in_specs=placed,
        out_specs=placed[0],
        check_vma=False,
    )
```
